512 devices in a mesh: gx: 8 (over x, core), gy: 8 (over y), gz: 8 (over z).
Axes of the slice: x: 4, y: 8, z: 8, core: 2. Of those that a mesh axis runs over, the one named last changes fastest.
Arguments:
- orbitals_in: float32 [128, 128, 128, 128], P('gx', 'gy', 'gz'), may hold values from -12 to 12
- potential: float32 [128, 128, 128], P('gx', 'gy', 'gz'), may hold values from 0 to 4
Outputs:
- orbitals: float32 [128, 128, 128, 128], P('gx', 'gy', 'gz')
- factor: float32 [128, 128], replicated
The draws below stay inside these ranges and needn't reach their ends.
All inputs are finite; a program needn't handle non-finite values.
Results may differ from the reference program's by a relative error of at most 0.0029.
Values sent between devices are 32-bit elements; how exact they have to be, the bound alone decides.
A program may use at most 64 MiB of HBM per device.

```python
import jax
import jax.numpy as jnp

K = 128
NX = 128
NY = 128
NZ = 128


def draw_orbitals_in(key, part):
    key_base = jax.random.fold_in(key, 11)
    key_noise = jax.random.fold_in(key, 23)
    key_order = jax.random.fold_in(key, 37)
    order = jax.random.permutation(key_order, K).astype(jnp.float32)
    grade = jnp.power(jnp.float32(0.002), order / jnp.float32(K - 1))
    base = jnp.clip(jax.random.normal(key_base, (NX, NY, NZ, 1), jnp.float32), -6.0, 6.0)
    noise = jnp.clip(jax.random.normal(key_noise, (NX, NY, NZ, K), jnp.float32), -6.0, 6.0)
    return (base + grade[None, None, None, :] * noise).astype(jnp.float32)


def levels(key, extent, shards, smallest, largest):
    factor_of = 1.0
    for dim, blocks in shards:
        draws = jax.random.uniform(jax.random.fold_in(jax.random.fold_in(key, 6), dim), (blocks,), jnp.float32, smallest / len(shards), largest / len(shards))
        factor_of = factor_of * jnp.repeat(jnp.exp(draws), extent[dim] // blocks).reshape((-1,) + (1,) * (len(extent) - 1 - dim))
    return factor_of


def setup_inputs(seed: int = 0) -> dict:
    streams_of = jax.random.split(jax.random.key(seed), 3)
    orbitals_in = draw_orbitals_in(jax.random.fold_in(streams_of[2], 71), 0)
    potential = jnp.clip(4.0 * jax.random.uniform(streams_of[1], (NX, NY, NZ), jnp.float32) ** levels(streams_of[1], (NX, NY, NZ), ((0, 8), (1, 8), (2, 8)), -0.2, 0.2), 0.0, 4.0)
    return {"orbitals_in": orbitals_in, "potential": potential}


SHIFT_CENTER = 5.0
HALF_WIDTH = 5.0

def apply_hamiltonian(padded, potential):
    center = padded[1:-1, 1:-1, 1:-1]
    beside = padded[2:, 1:-1, 1:-1] + padded[:-2, 1:-1, 1:-1]
    beside = beside + padded[1:-1, 2:, 1:-1] + padded[1:-1, :-2, 1:-1]
    beside = beside + padded[1:-1, 1:-1, 2:] + padded[1:-1, 1:-1, :-2]
    return (-0.5 * (beside - 6.0 * center) + potential[..., None] * center, center)

def pad_field(grid_field):
    return jnp.pad(grid_field, ((1, 1), (1, 1), (1, 1), (0, 0)))

def reference(orbitals_in, potential):
    image, center = apply_hamiltonian(pad_field(orbitals_in), potential)
    first_step = (image - SHIFT_CENTER * center) / HALF_WIDTH
    image_two, center_two = apply_hamiltonian(pad_field(first_step), potential)
    second = 2.0 * (image_two - SHIFT_CENTER * center_two) / HALF_WIDTH - orbitals_in
    points = NX * NY * NZ
    matrix = second.reshape(points, K)
    q_full, r_full = jnp.linalg.qr(matrix)
    diagonal = jnp.diagonal(r_full)
    signs = jnp.where(diagonal >= 0, 1.0, -1.0).astype(matrix.dtype)
    scale = jnp.sqrt(jnp.asarray(points, matrix.dtype))
    orbitals = (q_full * signs[None, :] * scale).reshape(NX, NY, NZ, K)
    factor = r_full * signs[:, None] / scale
    return (orbitals, factor)
```

```python
import functools

import jax
import jax.numpy as jnp
from jax import lax
from jax.experimental import pallas as pl
from jax.experimental.pallas import tpu as pltpu
from jax.sharding import PartitionSpec as P

AXES = ("gx", "gy", "gz")
HIGHEST = lax.Precision.HIGHEST
F32 = jnp.float32
MESH = pl.DeviceIdType.MESH


def position():
    return tuple(lax.axis_index(a) for a in AXES)


def moved(place, dim, index):
    return tuple(index if d == dim else place[d] for d in range(3))


def greet(place, sizes):
    barrier = pltpu.get_barrier_semaphore()
    for dim in range(3):
        for off in range(1, sizes[dim]):
            peer = lax.rem(place[dim] + off, sizes[dim])
            pl.semaphore_signal(
                barrier, inc=1, device_id=moved(place, dim, peer), device_id_type=MESH
            )
    pl.semaphore_wait(barrier, sum(n - 1 for n in sizes))


def line_copies(source, target, place, dim, size, send, recv):
    copies = []
    for off in range(1, size):
        peer = lax.rem(place[dim] + off, size)
        copies.append(
            pltpu.make_async_remote_copy(
                src_ref=source(peer),
                dst_ref=target,
                send_sem=send.at[off],
                recv_sem=recv.at[off],
                device_id=moved(place, dim, peer),
                device_id_type=MESH,
            )
        )
    for copy in copies:
        copy.start()
    return copies


def all_reduce(gram, out, place, sizes, part, land, send, recv):
    nx, ny, nz = sizes
    me = place[0]
    copies = line_copies(
        lambda peer: gram.at[peer], land.at[0, me], place, 0, nx, send.at[0], recv.at[0]
    )
    land[0, me] = gram[me]
    for stage in range(3):
        for copy in copies:
            copy.wait()
        total = land[stage, 0]
        for other in range(1, sizes[stage]):
            total = total + land[stage, other]
        if stage == 2:
            break
        dim = stage + 1
        part[stage] = total
        land[dim, place[dim]] = total
        copies = line_copies(
            lambda peer: part.at[stage],
            land.at[dim, place[dim]],
            place,
            dim,
            sizes[dim],
            send.at[dim],
            recv.at[dim],
        )
    part[2] = total
    out[me] = total
    copies = line_copies(
        lambda peer: part.at[2], out.at[me], place, 0, nx, send.at[3], recv.at[3]
    )
    for copy in copies:
        copy.wait()


def halo_exchange(field, low_z, high_z, faces, place, sizes, block, send, recv):
    bx, by, bz = block
    inner_x, inner_y = pl.ds(1, bx), pl.ds(1, by)
    moves = (
        (0, -1, field.at[1, inner_y], field.at[bx + 1, inner_y]),
        (0, 1, field.at[bx, inner_y], field.at[0, inner_y]),
        (1, -1, field.at[inner_x, 1], field.at[inner_x, by + 1]),
        (1, 1, field.at[inner_x, by], field.at[inner_x, 0]),
        (2, -1, faces.at[0], high_z),
        (2, 1, faces.at[1], low_z),
    )
    pairs = []
    for number, (dim, step, source, target) in enumerate(moves):
        index = place[dim]
        sends = index > 0 if step < 0 else index < sizes[dim] - 1
        gets = index < sizes[dim] - 1 if step < 0 else index > 0
        peer = lax.rem(index + step + sizes[dim], sizes[dim])
        copy = pltpu.make_async_remote_copy(
            src_ref=source,
            dst_ref=target,
            send_sem=send.at[number],
            recv_sem=recv.at[number],
            device_id=moved(place, dim, peer),
            device_id_type=MESH,
        )
        pairs.append((sends, gets, copy, target))
    for sends, gets, copy, target in pairs:
        pl.when(sends)(copy.start)

        @pl.when(jnp.logical_not(gets))
        def _():
            target[...] = jnp.zeros(target.shape, F32)

    def finish():
        for sends, gets, copy, target in pairs:
            pl.when(gets)(copy.wait_recv)
            pl.when(sends)(copy.wait_send)

    return finish


def pack_faces(field, faces, block):
    bx, by, bz = block

    def one(x, carry):
        faces[0, x] = field[x + 1, pl.ds(1, by), 0, :]
        faces[1, x] = field[x + 1, pl.ds(1, by), bz - 1, :]
        return carry

    lax.fori_loop(0, bx, one, 0)


def neighbour_sums(field, low_z, high_z, x, y, sub, bz):
    centre = field[x + 1, y + 1]
    beside = field[x, y + 1] + field[x + 2, y + 1]
    beside = beside + (field[x + 1, y] + field[x + 1, y + 2])
    below = jnp.where(sub == 0, low_z[x, pl.ds(y, 1), :], pltpu.roll(centre, 1, 0))
    above = jnp.where(
        sub == bz - 1, high_z[x, pl.ds(y, 1), :], pltpu.roll(centre, bz - 1, 0)
    )
    return centre, beside + (below + above)


def filter_kernel(
    sizes, orb, pot, second_out, gram_out,
    field, middle, low_z, high_z, faces, slab, gram, part, land,
    load_sem, store_sem, halo_send, halo_recv, line_send, line_recv,
):
    place = position()
    bx, by, bz, width = orb.shape
    block = (bx, by, bz)
    load = pltpu.make_async_copy(orb, field.at[pl.ds(1, bx), pl.ds(1, by)], load_sem)
    load.start()
    greet(place, sizes)
    load.wait()
    pack_faces(field, faces.at[0], block)
    finish = halo_exchange(
        field, low_z.at[0], high_z.at[0], faces.at[0], place, sizes, block,
        halo_send.at[0], halo_recv.at[0],
    )
    finish()
    sub = lax.broadcasted_iota(jnp.int32, (bz, width), 0)

    def first(x, carry):
        scale = 0.2 * pot[x] - 0.4
        for y in range(by):
            centre, beside = neighbour_sums(field, low_z.at[0], high_z.at[0], x, y, sub, bz)
            middle[x + 1, y + 1] = scale[:, y : y + 1] * centre - 0.1 * beside
        return carry

    lax.fori_loop(0, bx, first, 0)
    pack_faces(middle, faces.at[1], block)
    finish = halo_exchange(
        middle, low_z.at[1], high_z.at[1], faces.at[1], place, sizes, block,
        halo_send.at[1], halo_recv.at[1],
    )
    finish()

    def second(x, total):
        scale = 0.4 * pot[x] - 0.8
        for y in range(by):
            centre, beside = neighbour_sums(middle, low_z.at[1], high_z.at[1], x, y, sub, bz)
            slab[x, y] = scale[:, y : y + 1] * centre - 0.2 * beside - field[x + 1, y + 1]
        rows = slab[x].reshape(by * bz, width)
        return total + lax.dot_general(
            rows, rows, (((0,), (0,)), ((), ())), precision=HIGHEST,
            preferred_element_type=F32,
        )

    total = lax.fori_loop(0, bx, second, jnp.zeros((width, width), F32))
    store = pltpu.make_async_copy(slab, second_out, store_sem)
    store.start()
    gram[...] = total.reshape(gram.shape)
    all_reduce(gram, gram_out, place, sizes, part, land, line_send, line_recv)
    store.wait()


def reduce_kernel(sizes, gram_in, gram_out, gram, part, land, copy_sem, line_send, line_recv):
    place = position()
    greet(place, sizes)
    all_reduce(gram_in, gram_out, place, sizes, part, land, line_send, line_recv)


def spread(row, height=8):
    return jnp.broadcast_to(row, (height, row.shape[1]))


def inverse_factor(state, result):
    tiles, high, wide = state.shape
    lane = lax.broadcasted_iota(jnp.int32, (high, wide), 1)
    row = lax.broadcasted_iota(jnp.int32, (high, wide), 0)
    for p in range(tiles):
        j0 = p * high
        inside = (lane >= j0) & (lane < j0 + high)
        panel = state[p]
        columns = [jnp.broadcast_to(panel[:, j0 + t : j0 + t + 1], (high, wide)) for t in range(high)]
        d = [[spread(columns[t][i : i + 1]) if i >= t else None for t in range(high)] for i in range(high)]
        line = jnp.where(inside, jnp.where(lane - j0 == row, 1.0, 0.0), panel)
        lines = [spread(line[t : t + 1]) for t in range(high)]
        below = []
        for i in range(p + 1, tiles):
            other = state[i]
            parts = [
                jnp.broadcast_to(other[:, j0 + t : j0 + t + 1], (high, wide))
                for t in range(high)
            ]
            below.append([i, jnp.where(inside, 0.0, other), parts])
        block = None
        for t in range(high):
            rec = 1.0 / d[t][t]
            for i in range(t + 1, high):
                m = d[i][t] * rec
                for u in range(t + 1, i + 1):
                    d[i][u] = d[i][u] - m * d[u][t]
                lines[i] = lines[i] - m * lines[t]
            for entry in below:
                parts = entry[2]
                m = parts[t] * rec
                for u in range(t + 1, high):
                    parts[u] = parts[u] - m * d[u][t]
                entry[1] = entry[1] - m * lines[t]
            scaled = lines[t] * lax.rsqrt(d[t][t])
            block = scaled if block is None else jnp.where(row == t, scaled, block)
        for i, value, _ in below:
            state[i] = value
        result[p] = jnp.where(lane <= j0 + row, block, 0.0)


def product(a, b, dims):
    return lax.dot_general(
        a, b, (dims, ((), ())), precision=HIGHEST, preferred_element_type=F32
    )


def first_pass_kernel(points, second, gram, q_out, back_out, gram_out, state, back):
    width = gram.shape[-1]
    state[...] = gram[...] * (1.0 / points)
    inverse_factor(state, back)
    lower = back[...].reshape(width, width)
    back_out[...] = lower

    def one(x, total):
        rows = second[x].reshape(-1, width)
        q = product(rows, lower, ((1,), (1,)))
        q_out[x] = q.reshape(q_out.shape[1:])
        return total + product(q, q, ((0,), (0,)))

    total = lax.fori_loop(0, second.shape[0], one, jnp.zeros((width, width), F32))
    gram_out[...] = total.reshape(gram_out.shape)


def last_pass_kernel(points, q_in, gram, back_one, gram_one, q_out, factor, state, back):
    width = gram.shape[-1]
    state[...] = gram[...] * (1.0 / points)
    inverse_factor(state, back)
    lower = back[...].reshape(width, width)

    def one(x, carry):
        rows = q_in[x].reshape(-1, width)
        q_out[x] = product(rows, lower, ((1,), (1,))).reshape(q_out.shape[1:])
        return carry

    lax.fori_loop(0, q_in.shape[0], one, 0)
    whole = product(lower, back_one[...], ((1,), (0,)))
    r = product(whole, gram_one[...].reshape(width, width) * (1.0 / points), ((1,), (0,)))
    at = lax.broadcasted_iota(jnp.int32, r.shape, 0) <= lax.broadcasted_iota(jnp.int32, r.shape, 1)
    factor[...] = jnp.where(at, r, 0.0)


def local(sizes, orbitals_in, potential):
    bx, by, bz, width = orbitals_in.shape
    points = bx * by * bz * sizes[0] * sizes[1] * sizes[2]
    nx = sizes[0]
    rows = width // nx
    longest = max(sizes)
    vmem = pl.BlockSpec(memory_space=pltpu.VMEM)
    anywhere = pl.BlockSpec(memory_space=pl.ANY)
    pot = jnp.transpose(potential, (0, 2, 1))
    chunks = jax.ShapeDtypeStruct((nx, rows, width), F32)
    tiles = jax.ShapeDtypeStruct((width // 8, 8, width), F32)
    field_shape = jax.ShapeDtypeStruct(orbitals_in.shape, F32)
    square = jax.ShapeDtypeStruct((width, width), F32)
    line_scratch = [
        pltpu.VMEM((nx, rows, width), F32),
        pltpu.VMEM((3, rows, width), F32),
        pltpu.VMEM((3, longest, rows, width), F32),
    ]
    line_sems = [pltpu.SemaphoreType.DMA((4, longest)), pltpu.SemaphoreType.DMA((4, longest))]
    second, gram_one = pl.pallas_call(
        functools.partial(filter_kernel, sizes),
        out_shape=(field_shape, chunks),
        in_specs=[anywhere, vmem],
        out_specs=(anywhere, vmem),
        scratch_shapes=[
            pltpu.VMEM((bx + 2, by + 2, bz, width), F32),
            pltpu.VMEM((bx + 2, by + 2, bz, width), F32),
            pltpu.VMEM((2, bx, by, width), F32),
            pltpu.VMEM((2, bx, by, width), F32),
            pltpu.VMEM((2, 2, bx, by, width), F32),
            pltpu.VMEM((bx, by, bz, width), F32),
            *line_scratch,
            pltpu.SemaphoreType.DMA(()),
            pltpu.SemaphoreType.DMA(()),
            pltpu.SemaphoreType.DMA((2, 6)),
            pltpu.SemaphoreType.DMA((2, 6)),
            *line_sems,
        ],
        compiler_params=pltpu.CompilerParams(collective_id=0, has_side_effects=True),
        name="filter_gram",
    )(orbitals_in, pot)
    q_one, back_one, gram_local = pl.pallas_call(
        functools.partial(first_pass_kernel, points),
        out_shape=(field_shape, square, tiles),
        in_specs=[vmem, vmem],
        out_specs=(vmem, vmem, vmem),
        scratch_shapes=[pltpu.VMEM(tiles.shape, F32), pltpu.VMEM(tiles.shape, F32)],
        name="first_pass",
    )(second, gram_one.reshape(tiles.shape))
    gram_two = pl.pallas_call(
        functools.partial(reduce_kernel, sizes),
        out_shape=chunks,
        in_specs=[vmem],
        out_specs=vmem,
        scratch_shapes=[*line_scratch, pltpu.SemaphoreType.DMA(()), *line_sems],
        compiler_params=pltpu.CompilerParams(collective_id=1, has_side_effects=True),
        name="gram_reduce",
    )(gram_local.reshape(chunks.shape))
    orbitals, factor = pl.pallas_call(
        functools.partial(last_pass_kernel, points),
        out_shape=(field_shape, square),
        in_specs=[vmem, vmem, vmem, vmem],
        out_specs=(vmem, vmem),
        scratch_shapes=[pltpu.VMEM(tiles.shape, F32), pltpu.VMEM(tiles.shape, F32)],
        name="last_pass",
    )(q_one, gram_two.reshape(tiles.shape), back_one, gram_one)
    return orbitals, factor


def solution(mesh):
    sizes = tuple(mesh.shape[a] for a in AXES)
    spec = P("gx", "gy", "gz", None)
    return jax.shard_map(
        functools.partial(local, sizes),
        mesh=mesh,
        in_specs=(spec, P("gx", "gy", "gz")),
        out_specs=(spec, P()),
        check_vma=False,
    )
```

```python
import functools

import jax
import jax.numpy as jnp
from jax import lax
from jax.experimental import pallas as pl
from jax.experimental.pallas import tpu as pltpu
from jax.sharding import PartitionSpec as P

AXES = ("gx", "gy", "gz")
HIGHEST = lax.Precision.HIGHEST
F32 = jnp.float32
MESH = pl.DeviceIdType.MESH


def position():
    return tuple(lax.axis_index(a) for a in AXES)


def moved(place, dim, index):
    return tuple(index if d == dim else place[d] for d in range(3))


def greet(place, sizes):
    barrier = pltpu.get_barrier_semaphore()
    for dim in range(3):
        for off in range(1, sizes[dim]):
            peer = lax.rem(place[dim] + off, sizes[dim])
            pl.semaphore_signal(
                barrier, inc=1, device_id=moved(place, dim, peer), device_id_type=MESH
            )
    pl.semaphore_wait(barrier, sum(n - 1 for n in sizes))


def line_copies(source, target, place, dim, size, send, recv):
    copies = []
    for off in range(1, size):
        peer = lax.rem(place[dim] + off, size)
        copies.append(
            pltpu.make_async_remote_copy(
                src_ref=source(peer),
                dst_ref=target,
                send_sem=send.at[off],
                recv_sem=recv.at[off],
                device_id=moved(place, dim, peer),
                device_id_type=MESH,
            )
        )
    for copy in copies:
        copy.start()
    return copies


def two_sum(a, b):
    total = a + b
    back = total - a
    return total, (a - (total - back)) + (b - back)


def pair_add(high, low, other_high, other_low):
    high, error = two_sum(high, other_high)
    return high, low + (error + other_low)


def normal_pair(high, low):
    total = high + low
    return total, low - (total - high)


def all_reduce(gram, out, place, sizes, part, land, send, recv):
    nx, ny, nz = sizes
    me = place[0]
    rows = gram.shape[1] // 2
    copies = line_copies(
        lambda peer: gram.at[peer], land.at[0, me], place, 0, nx, send.at[0], recv.at[0]
    )
    land[0, me] = gram[me]
    for stage in range(3):
        for copy in copies:
            copy.wait()
        high, low = land[stage, 0, :rows], land[stage, 0, rows:]
        for other in range(1, sizes[stage]):
            high, low = pair_add(
                high, low, land[stage, other, :rows], land[stage, other, rows:]
            )
        high, low = normal_pair(high, low)
        if stage == 2:
            break
        dim = stage + 1
        for target in (part.at[stage], land.at[dim, place[dim]]):
            target[:rows] = high
            target[rows:] = low
        copies = line_copies(
            lambda peer: part.at[stage],
            land.at[dim, place[dim]],
            place,
            dim,
            sizes[dim],
            send.at[dim],
            recv.at[dim],
        )
    for target in (part.at[2], out.at[me]):
        target[:rows] = high
        target[rows:] = low
    copies = line_copies(
        lambda peer: part.at[2], out.at[me], place, 0, nx, send.at[3], recv.at[3]
    )
    for copy in copies:
        copy.wait()


def halo_exchange(field, low_z, high_z, faces, place, sizes, block, send, recv):
    bx, by, bz = block
    inner_x, inner_y = pl.ds(1, bx), pl.ds(1, by)
    moves = (
        (0, -1, field.at[1, inner_y], field.at[bx + 1, inner_y]),
        (0, 1, field.at[bx, inner_y], field.at[0, inner_y]),
        (1, -1, field.at[inner_x, 1], field.at[inner_x, by + 1]),
        (1, 1, field.at[inner_x, by], field.at[inner_x, 0]),
        (2, -1, faces.at[0], high_z),
        (2, 1, faces.at[1], low_z),
    )
    pairs = []
    for number, (dim, step, source, target) in enumerate(moves):
        index = place[dim]
        sends = index > 0 if step < 0 else index < sizes[dim] - 1
        gets = index < sizes[dim] - 1 if step < 0 else index > 0
        peer = lax.rem(index + step + sizes[dim], sizes[dim])
        copy = pltpu.make_async_remote_copy(
            src_ref=source,
            dst_ref=target,
            send_sem=send.at[number],
            recv_sem=recv.at[number],
            device_id=moved(place, dim, peer),
            device_id_type=MESH,
        )
        pairs.append((sends, gets, copy, target))
    for sends, gets, copy, target in pairs:
        pl.when(sends)(copy.start)

        @pl.when(jnp.logical_not(gets))
        def _():
            target[...] = jnp.zeros(target.shape, F32)

    def finish():
        for sends, gets, copy, target in pairs:
            pl.when(gets)(copy.wait_recv)
            pl.when(sends)(copy.wait_send)

    return finish


def pack_faces(field, faces, block):
    bx, by, bz = block

    def one(x, carry):
        faces[0, x] = field[x + 1, pl.ds(1, by), 0, :]
        faces[1, x] = field[x + 1, pl.ds(1, by), bz - 1, :]
        return carry

    lax.fori_loop(0, bx, one, 0)


def neighbour_sums(field, low_z, high_z, x, y, sub, bz):
    centre = field[x + 1, y + 1]
    beside = field[x, y + 1] + field[x + 2, y + 1]
    beside = beside + (field[x + 1, y] + field[x + 1, y + 2])
    below = jnp.where(sub == 0, low_z[x, pl.ds(y, 1), :], pltpu.roll(centre, 1, 0))
    above = jnp.where(
        sub == bz - 1, high_z[x, pl.ds(y, 1), :], pltpu.roll(centre, bz - 1, 0)
    )
    return centre, beside + (below + above)


def add_gram(sums, rows):
    width = rows.shape[1]
    one = rows.astype(jnp.bfloat16)
    rest = rows - one.astype(F32)
    two = rest.astype(jnp.bfloat16)
    three = (rest - two.astype(F32)).astype(jnp.bfloat16)
    dims = (((0,), (0,)), ((), ()))
    first = lax.dot_general(
        one, jnp.concatenate([one, two, three], axis=1), dims, preferred_element_type=F32
    )
    later = lax.dot_general(
        two, jnp.concatenate([two, three], axis=1), dims, preferred_element_type=F32
    )
    high, error = two_sum(sums[0], first[:, :width])
    sums[0] = high
    sums[1] = sums[1] + (error + later[:, :width])
    sums[2] = sums[2] + (first[:, width : 2 * width] + (first[:, 2 * width :] + later[:, width:]))


def filter_kernel(
    sizes, orb, pot, second_out, gram_out,
    field, middle, low_z, high_z, faces, slab, turned, sums, gram, part, land,
    load_sem, store_sem, halo_send, halo_recv, line_send, line_recv,
):
    place = position()
    bx, by, bz, width = orb.shape
    block = (bx, by, bz)
    load = pltpu.make_async_copy(orb, field.at[pl.ds(1, bx), pl.ds(1, by)], load_sem)
    load.start()

    def turn(x, carry):
        turned[x] = pot[x].T
        return carry

    lax.fori_loop(0, bx, turn, 0)
    greet(place, sizes)
    load.wait()
    pack_faces(field, faces.at[0], block)
    finish = halo_exchange(
        field, low_z.at[0], high_z.at[0], faces.at[0], place, sizes, block,
        halo_send.at[0], halo_recv.at[0],
    )
    finish()
    sub = lax.broadcasted_iota(jnp.int32, (bz, width), 0)

    def first(x, carry):
        scale = 0.2 * turned[x] - 0.4
        for y in range(by):
            centre, beside = neighbour_sums(field, low_z.at[0], high_z.at[0], x, y, sub, bz)
            middle[x + 1, y + 1] = scale[:, y : y + 1] * centre - 0.1 * beside
        return carry

    lax.fori_loop(0, bx, first, 0)
    pack_faces(middle, faces.at[1], block)
    finish = halo_exchange(
        middle, low_z.at[1], high_z.at[1], faces.at[1], place, sizes, block,
        halo_send.at[1], halo_recv.at[1],
    )
    finish()

    sums[...] = jnp.zeros(sums.shape, F32)

    def second(x, carry):
        scale = 0.4 * turned[x] - 0.8
        for y in range(by):
            centre, beside = neighbour_sums(middle, low_z.at[1], high_z.at[1], x, y, sub, bz)
            slab[x, y] = scale[:, y : y + 1] * centre - 0.2 * beside - field[x + 1, y + 1]
        add_gram(sums, slab[x].reshape(by * bz, width))
        return carry

    lax.fori_loop(0, bx, second, 0)
    store = pltpu.make_async_copy(slab, second_out, store_sem)
    store.start()
    cross = sums[2]
    high, low = two_sum(sums[0], sums[1] + (cross + cross.T))
    rows = gram.shape[1] // 2
    for chunk in range(gram.shape[0]):
        gram[chunk, :rows] = high[chunk * rows : (chunk + 1) * rows]
        gram[chunk, rows:] = low[chunk * rows : (chunk + 1) * rows]
    all_reduce(gram, gram_out, place, sizes, part, land, line_send, line_recv)
    store.wait()


def spread(row, height=8):
    return jnp.broadcast_to(row, (height, row.shape[1]))


def inverse_factor(state, result):
    tiles, high, wide = state.shape
    lane = lax.broadcasted_iota(jnp.int32, (high, wide), 1)
    row = lax.broadcasted_iota(jnp.int32, (high, wide), 0)
    for p in range(tiles):
        j0 = p * high
        inside = (lane >= j0) & (lane < j0 + high)
        panel = state[p]
        columns = [jnp.broadcast_to(panel[:, j0 + t : j0 + t + 1], (high, wide)) for t in range(high)]
        d = [[spread(columns[t][i : i + 1]) if i >= t else None for t in range(high)] for i in range(high)]
        line = jnp.where(inside, jnp.where(lane - j0 == row, 1.0, 0.0), panel)
        lines = [spread(line[t : t + 1]) for t in range(high)]
        below = []
        for i in range(p + 1, tiles):
            other = state[i]
            parts = [
                jnp.broadcast_to(other[:, j0 + t : j0 + t + 1], (high, wide))
                for t in range(high)
            ]
            below.append([i, jnp.where(inside, 0.0, other), parts])
        block = None
        for t in range(high):
            rec = 1.0 / d[t][t]
            for i in range(t + 1, high):
                m = d[i][t] * rec
                for u in range(t + 1, i + 1):
                    d[i][u] = d[i][u] - m * d[u][t]
                lines[i] = lines[i] - m * lines[t]
            for entry in below:
                parts = entry[2]
                m = parts[t] * rec
                for u in range(t + 1, high):
                    parts[u] = parts[u] - m * d[u][t]
                entry[1] = entry[1] - m * lines[t]
            scaled = lines[t] * lax.rsqrt(d[t][t])
            block = scaled if block is None else jnp.where(row == t, scaled, block)
        for i, value, _ in below:
            state[i] = value
        result[p] = jnp.where(lane <= j0 + row, block, 0.0)


def product(a, b, dims):
    return lax.dot_general(
        a, b, (dims, ((), ())), precision=HIGHEST, preferred_element_type=F32
    )


def power_above(value):
    power = jnp.full(value.shape, 2.0**-32, F32)
    for step in (32, 16, 8, 4, 2, 1):
        more = power * 2.0**step
        power = jnp.where(power * 2.0 ** (step - 1) < value, more, power)
    return power


def slices(value, count):
    parts = []
    for k in range(count):
        step = 2.0 ** (8 + 9 * k)
        piece = jnp.round(value * step) * (1.0 / step)
        parts.append(piece.astype(jnp.bfloat16))
        value = value - piece
    return parts, value


def exact_dot(a, b):
    return lax.dot_general(
        a, b, (((1,), (0,)), ((), ())), preferred_element_type=F32
    )


def upper_half(square):
    row = lax.broadcasted_iota(jnp.int32, square.shape, 0)
    column = lax.broadcasted_iota(jnp.int32, square.shape, 1)
    return jnp.where(row < column, square, jnp.where(row == column, 0.5 * square, 0.0))


def final_kernel(
    points, second, gram, q_out, factor, block, state, back, load_sem, store_sem
):
    load = pltpu.make_async_copy(second, block, load_sem)
    load.start()
    nx, rows, width = gram.shape[0], gram.shape[1] // 2, gram.shape[2]
    high = jnp.concatenate([gram[c, :rows] for c in range(nx)], axis=0) * (1.0 / points)
    low = jnp.concatenate([gram[c, rows:] for c in range(nx)], axis=0) * (1.0 / points)
    row = lax.broadcasted_iota(jnp.int32, high.shape, 0)
    column = lax.broadcasted_iota(jnp.int32, high.shape, 1)
    diagonal = jnp.where(row == column, high, 0.0)
    down = 1.0 / power_above(jnp.sqrt(jnp.sum(diagonal, axis=1, keepdims=True)))
    across = 1.0 / power_above(jnp.sqrt(jnp.sum(diagonal, axis=0, keepdims=True)))
    high = high * down * across
    low = low * down * across
    state[...] = high.reshape(state.shape)
    inverse_factor(state, back)
    lower = back[...].reshape(width, width)
    size = power_above(jnp.max(jnp.abs(lower), axis=1, keepdims=True))
    b, rest = slices(lower * (1.0 / size), 3)
    lower = lower - rest * size
    g, rest = slices(high, 3)
    g.append((rest + low).astype(jnp.bfloat16))
    image = exact_dot(b[0], g[0])
    image = image + (exact_dot(b[0], g[1]) + exact_dot(b[1], g[0]))
    image = image + (exact_dot(b[0], g[2]) + exact_dot(b[1], g[1]) + exact_dot(b[2], g[0]))
    image = image + (exact_dot(b[0], g[3]) + exact_dot(b[1], g[2]) + exact_dot(b[2], g[1]))
    image = image * size
    error = product(image, lower, ((1,), (1,))) - jnp.where(row == column, 1.0, 0.0)
    x = upper_half(error)
    for _ in range(2):
        x = upper_half(error - product(x, x, ((0,), (0,))))
    both = jnp.concatenate([lower, image], axis=1)
    x2 = product(x, x, ((1,), (0,)))
    both = both - product(x, both, ((0,), (0,)))
    both = both + product(x2, both, ((0,), (0,)))
    lower = both[:, :width] * across
    factor[...] = jnp.where(row <= column, both[:, width:] * (1.0 / across), 0.0)
    load.wait()

    def one(x, carry):
        rows = block[x].reshape(-1, width)
        block[x] = product(rows, lower, ((1,), (1,))).reshape(block.shape[1:])
        pltpu.make_async_copy(block.at[x], q_out.at[x], store_sem.at[x]).start()
        return carry

    lax.fori_loop(0, block.shape[0], one, 0)

    def drain(x, carry):
        pltpu.make_async_copy(block.at[x], q_out.at[x], store_sem.at[x]).wait()
        return carry

    lax.fori_loop(0, block.shape[0], drain, 0)


def local(sizes, orbitals_in, potential):
    bx, by, bz, width = orbitals_in.shape
    points = bx * by * bz * sizes[0] * sizes[1] * sizes[2]
    nx = sizes[0]
    rows = width // nx
    longest = max(sizes)
    vmem = pl.BlockSpec(memory_space=pltpu.VMEM)
    anywhere = pl.BlockSpec(memory_space=pl.ANY)
    chunks = jax.ShapeDtypeStruct((nx, 2 * rows, width), F32)
    tiles = (width // 8, 8, width)
    field_shape = jax.ShapeDtypeStruct(orbitals_in.shape, F32)
    square = jax.ShapeDtypeStruct((width, width), F32)
    second, gram = pl.pallas_call(
        functools.partial(filter_kernel, sizes),
        out_shape=(field_shape, chunks),
        in_specs=[anywhere, vmem],
        out_specs=(anywhere, vmem),
        scratch_shapes=[
            pltpu.VMEM((bx + 2, by + 2, bz, width), F32),
            pltpu.VMEM((bx + 2, by + 2, bz, width), F32),
            pltpu.VMEM((2, bx, by, width), F32),
            pltpu.VMEM((2, bx, by, width), F32),
            pltpu.VMEM((2, 2, bx, by, width), F32),
            pltpu.VMEM((bx, by, bz, width), F32),
            pltpu.VMEM((bx, bz, by), F32),
            pltpu.VMEM((3, width, width), F32),
            pltpu.VMEM(chunks.shape, F32),
            pltpu.VMEM((3, 2 * rows, width), F32),
            pltpu.VMEM((3, longest, 2 * rows, width), F32),
            pltpu.SemaphoreType.DMA(()),
            pltpu.SemaphoreType.DMA(()),
            pltpu.SemaphoreType.DMA((2, 6)),
            pltpu.SemaphoreType.DMA((2, 6)),
            pltpu.SemaphoreType.DMA((4, longest)),
            pltpu.SemaphoreType.DMA((4, longest)),
        ],
        compiler_params=pltpu.CompilerParams(collective_id=0, has_side_effects=True),
        name="filter_gram",
    )(orbitals_in, potential)
    return pl.pallas_call(
        functools.partial(final_kernel, points),
        out_shape=(field_shape, square),
        in_specs=[anywhere, vmem],
        out_specs=(anywhere, vmem),
        scratch_shapes=[
            pltpu.VMEM(orbitals_in.shape, F32),
            pltpu.VMEM(tiles, F32),
            pltpu.VMEM(tiles, F32),
            pltpu.SemaphoreType.DMA(()),
            pltpu.SemaphoreType.DMA((bx,)),
        ],
        name="factor_apply",
    )(second, gram)


def solution(mesh):
    sizes = tuple(mesh.shape[a] for a in AXES)
    spec = P("gx", "gy", "gz", None)
    return jax.shard_map(
        functools.partial(local, sizes),
        mesh=mesh,
        in_specs=(spec, P("gx", "gy", "gz")),
        out_specs=(spec, P()),
        check_vma=False,
    )
```

```python
import functools

import jax
import jax.numpy as jnp
from jax import lax
from jax.experimental import pallas as pl
from jax.experimental.pallas import tpu as pltpu
from jax.sharding import PartitionSpec as P

AXES = ("gx", "gy", "gz")
HIGHEST = lax.Precision.HIGHEST
F32 = jnp.float32
MESH = pl.DeviceIdType.MESH


def position():
    return tuple(lax.axis_index(a) for a in AXES)


def moved(place, dim, index):
    return tuple(index if d == dim else place[d] for d in range(3))


def greet(place, sizes):
    barrier = pltpu.get_barrier_semaphore()
    for dim in range(3):
        for off in range(1, sizes[dim]):
            peer = lax.rem(place[dim] + off, sizes[dim])
            pl.semaphore_signal(
                barrier, inc=1, device_id=moved(place, dim, peer), device_id_type=MESH
            )
    return lambda: pl.semaphore_wait(barrier, sum(n - 1 for n in sizes))


def line_copies(source, target, place, dim, size, send, recv):
    copies = []
    for off in range(1, size):
        peer = lax.rem(place[dim] + off, size)
        copies.append(
            pltpu.make_async_remote_copy(
                src_ref=source(peer),
                dst_ref=target,
                send_sem=send.at[off],
                recv_sem=recv.at[off],
                device_id=moved(place, dim, peer),
                device_id_type=MESH,
            )
        )
    for copy in copies:
        copy.start()
    return copies


def two_sum(a, b):
    total = a + b
    back = total - a
    return total, (a - (total - back)) + (b - back)


def pair_add(high, low, other_high, other_low):
    high, error = two_sum(high, other_high)
    return high, low + (error + other_low)


def packed(square):
    half = square.shape[0] // 2
    top, bottom = square[:half], square[half:]
    row = lax.broadcasted_iota(jnp.int32, top.shape, 0)
    lane = lax.broadcasted_iota(jnp.int32, top.shape, 1)
    rest = jnp.sum(jnp.where(lane == row + half, bottom, 0.0), axis=0, keepdims=True)
    return jnp.where(lane < row, pltpu.roll(bottom, half, 1), top), rest


def unpacked(rows, rest):
    half, width = rows.shape
    both = jnp.concatenate([rows, pltpu.roll(rows, half, 1)], axis=0)
    turned = both.T
    row = lax.broadcasted_iota(jnp.int32, both.shape, 0)
    lane = lax.broadcasted_iota(jnp.int32, both.shape, 1)
    take = ((row < half) & (lane >= row)) | ((row >= half) & (lane >= half) & (lane < row))
    full = jnp.where(take, both, turned)
    return jnp.where((row >= half) & (lane == row), jnp.broadcast_to(rest, both.shape), full)


def sum_slots(slots, count, rows):
    pairs = []
    for high_at, low_at in (
        (pl.ds(0, rows), pl.ds(rows, rows)),
        (pl.ds(2 * rows, 1), pl.ds(2 * rows + 1, 1)),
    ):
        high, low = slots[0, high_at], slots[0, low_at]
        for other in range(1, count):
            high, low = pair_add(high, low, slots[other, high_at], slots[other, low_at])
        pairs += [(high_at, high), (low_at, low)]
    return pairs


def all_reduce(gram, out, place, sizes, part, land, send, recv):
    nx, ny, nz = sizes
    me = place[0]
    rows = gram.shape[1] // 2 - 1
    copies = line_copies(
        lambda peer: gram.at[peer], land.at[0, me], place, 0, nx, send.at[0], recv.at[0]
    )
    land[0, me] = gram[me]
    for stage in range(3):
        for copy in copies:
            copy.wait()
        pairs = sum_slots(land.at[stage], sizes[stage], rows)
        if stage == 2:
            break
        dim = stage + 1
        for target in (part.at[stage], land.at[dim, place[dim]]):
            for at, value in pairs:
                target[at] = value
        copies = line_copies(
            lambda peer: part.at[stage],
            land.at[dim, place[dim]],
            place,
            dim,
            sizes[dim],
            send.at[dim],
            recv.at[dim],
        )
    for target in (part.at[2], out.at[me]):
        for at, value in pairs:
            target[at] = value
    copies = line_copies(
        lambda peer: part.at[2], out.at[me], place, 0, nx, send.at[3], recv.at[3]
    )
    for copy in copies:
        copy.wait()


def halo_exchange(source, first, field, low_z, high_z, faces, place, sizes, block, send, recv, pack):
    bx, by, bz = block
    inner_x, inner_y = pl.ds(1, bx), pl.ds(1, by)
    from_x, from_y = pl.ds(first, bx), pl.ds(first, by)
    moves = (
        (0, -1, source.at[first, from_y], field.at[bx + 1, inner_y]),
        (0, 1, source.at[first + bx - 1, from_y], field.at[0, inner_y]),
        (1, -1, source.at[from_x, first], field.at[inner_x, by + 1]),
        (1, 1, source.at[from_x, first + by - 1], field.at[inner_x, 0]),
        (2, -1, faces.at[0], high_z),
        (2, 1, faces.at[1], low_z),
    )
    pairs = []
    for number, (dim, step, source, target) in enumerate(moves):
        index = place[dim]
        sends = index > 0 if step < 0 else index < sizes[dim] - 1
        gets = index < sizes[dim] - 1 if step < 0 else index > 0
        peer = lax.rem(index + step + sizes[dim], sizes[dim])
        copy = pltpu.make_async_remote_copy(
            src_ref=source,
            dst_ref=target,
            send_sem=send.at[number],
            recv_sem=recv.at[number],
            device_id=moved(place, dim, peer),
            device_id_type=MESH,
        )
        pairs.append((sends, gets, copy, target))
    for sends, gets, copy, target in pairs[:4]:
        pl.when(sends)(copy.start)
    pack()
    for sends, gets, copy, target in pairs[4:]:
        pl.when(sends)(copy.start)
    for sends, gets, copy, target in pairs:

        @pl.when(jnp.logical_not(gets))
        def _():
            target[...] = jnp.zeros(target.shape, F32)

    def finish():
        for sends, gets, copy, target in pairs:
            pl.when(gets)(copy.wait_recv)
            pl.when(sends)(copy.wait_send)

    return finish


def pack_faces(field, faces, block):
    bx, by, bz = block

    def one(x, carry):
        faces[0, x] = field[x + 1, pl.ds(1, by), 0, :]
        faces[1, x] = field[x + 1, pl.ds(1, by), bz - 1, :]
        return carry

    lax.fori_loop(0, bx, one, 0)


def neighbour_sums(field, low_z, high_z, x, y, sub, bz):
    centre = field[x + 1, y + 1]
    beside = field[x, y + 1] + field[x + 2, y + 1]
    beside = beside + (field[x + 1, y] + field[x + 1, y + 2])
    below = jnp.where(sub == 0, low_z[x, pl.ds(y, 1), :], pltpu.roll(centre, 1, 0))
    above = jnp.where(
        sub == bz - 1, high_z[x, pl.ds(y, 1), :], pltpu.roll(centre, bz - 1, 0)
    )
    return centre, beside + (below + above)


def add_gram(sums, rows, pieces):
    width = rows.shape[1]
    one = rows.astype(jnp.bfloat16)
    wide = one.astype(F32)
    rest = rows - wide
    two = rest.astype(jnp.bfloat16)
    three = (rest - two.astype(F32)).astype(jnp.bfloat16)
    for k, piece in enumerate((one, two, three)):
        pieces[:, k * width : (k + 1) * width] = piece
    dims = (((0,), (0,)), ((), ()))
    first = lax.dot_general(
        one, jnp.concatenate([one, two, three], axis=1), dims, preferred_element_type=F32
    )
    later = lax.dot_general(
        two, jnp.concatenate([two, three], axis=1), dims, preferred_element_type=F32
    )
    squares = jnp.sum(wide * wide, axis=0, keepdims=True)
    row = lax.broadcasted_iota(jnp.int32, (width, width), 0)
    lane = lax.broadcasted_iota(jnp.int32, (width, width), 1)
    top = jnp.where(row == lane, jnp.broadcast_to(squares, row.shape), first[:, :width])
    high, error = two_sum(sums[0], top)
    sums[0] = high
    sums[1] = sums[1] + (error + later[:, :width])
    sums[2] = sums[2] + (first[:, width : 2 * width] + (first[:, 2 * width :] + later[:, width:]))


def filter_kernel(
    sizes, orb, pot_in, slices_out, gram_out,
    field, middle, low_z, high_z, faces, pieces, pot, turned, sums, gram, part, land,
    load_sem, store_sem, halo_send, halo_recv, line_send, line_recv,
):
    place = position()
    bx, by, bz, width = orb.shape
    block = (bx, by, bz)
    met = greet(place, sizes)
    load = pltpu.make_async_copy(orb, field.at[pl.ds(1, bx), pl.ds(1, by)], load_sem.at[0])
    load.start()
    load_pot = pltpu.make_async_copy(pot_in, pot, load_sem.at[1])
    load_pot.start()
    met()

    def pack_first():
        load.wait()
        pack_faces(field, faces.at[0], block)

    finish = halo_exchange(
        orb, 0, field, low_z.at[0], high_z.at[0], faces.at[0], place, sizes, block,
        halo_send.at[0], halo_recv.at[0], pack_first,
    )
    load_pot.wait()

    def turn(x, carry):
        turned[x] = pot[x].T
        return carry

    lax.fori_loop(0, bx, turn, 0)
    finish()
    sub = lax.broadcasted_iota(jnp.int32, (bz, width), 0)

    def first(x, carry):
        scale = 0.2 * turned[x] - 0.4
        for y in range(by):
            centre, beside = neighbour_sums(field, low_z.at[0], high_z.at[0], x, y, sub, bz)
            middle[x + 1, y + 1] = scale[:, y : y + 1] * centre - 0.1 * beside
        return carry

    lax.fori_loop(0, bx, first, 0)
    finish = halo_exchange(
        middle, 1, middle, low_z.at[1], high_z.at[1], faces.at[1], place, sizes, block,
        halo_send.at[1], halo_recv.at[1], lambda: pack_faces(middle, faces.at[1], block),
    )
    sums[...] = jnp.zeros(sums.shape, F32)
    finish()

    def second(x, carry):
        scale = 0.4 * turned[x] - 0.8
        lines = []
        for y in range(by):
            centre, beside = neighbour_sums(middle, low_z.at[1], high_z.at[1], x, y, sub, bz)
            lines.append(scale[:, y : y + 1] * centre - 0.2 * beside - field[x + 1, y + 1])
        add_gram(sums, jnp.concatenate(lines, axis=0), pieces.at[x])
        return carry

    lax.fori_loop(0, bx, second, 0)
    store = pltpu.make_async_copy(pieces, slices_out, store_sem)
    store.start()
    cross = sums[2]
    high, low = two_sum(sums[0], sums[1] + (cross + cross.T))
    rows = gram.shape[1] // 2 - 1
    for value, at, alone in ((high, 0, 2 * rows), (low, rows, 2 * rows + 1)):
        value, rest = packed(value)
        for chunk in range(gram.shape[0]):
            gram[chunk, at : at + rows] = value[chunk * rows : (chunk + 1) * rows]
            gram[chunk, alone : alone + 1] = rest
    all_reduce(gram, gram_out, place, sizes, part, land, line_send, line_recv)
    store.wait()


def spread(row, height=8):
    return jnp.broadcast_to(row, (height, row.shape[1]))


def inverse_factor(state, result):
    tiles, high, wide = state.shape
    lane = lax.broadcasted_iota(jnp.int32, (high, wide), 1)
    row = lax.broadcasted_iota(jnp.int32, (high, wide), 0)
    for p in range(tiles):
        j0 = p * high
        inside = (lane >= j0) & (lane < j0 + high)
        panel = state[p]
        columns = [jnp.broadcast_to(panel[:, j0 + t : j0 + t + 1], (high, wide)) for t in range(high)]
        d = [[spread(columns[t][i : i + 1]) if i >= t else None for t in range(high)] for i in range(high)]
        line = jnp.where(inside, jnp.where(lane - j0 == row, 1.0, 0.0), panel)
        lines = [spread(line[t : t + 1]) for t in range(high)]
        below = []
        for i in range(p + 1, tiles):
            other = state[i]
            parts = [
                jnp.broadcast_to(other[:, j0 + t : j0 + t + 1], (high, wide))
                for t in range(high)
            ]
            below.append([i, jnp.where(inside, 0.0, other), parts])
        block = None
        for t in range(high):
            rec = 1.0 / d[t][t]
            for i in range(t + 1, high):
                m = d[i][t] * rec
                for u in range(t + 1, i + 1):
                    d[i][u] = d[i][u] - m * d[u][t]
                lines[i] = lines[i] - m * lines[t]
            for entry in below:
                parts = entry[2]
                m = parts[t] * rec
                for u in range(t + 1, high):
                    parts[u] = parts[u] - m * d[u][t]
                entry[1] = entry[1] - m * lines[t]
            scaled = lines[t] * lax.rsqrt(d[t][t])
            block = scaled if block is None else jnp.where(row == t, scaled, block)
        for i, value, _ in below:
            state[i] = value
        result[p] = jnp.where(lane <= j0 + row, block, 0.0)


def product(a, b, dims):
    return lax.dot_general(
        a, b, (dims, ((), ())), precision=HIGHEST, preferred_element_type=F32
    )


def power_above(value):
    power = jnp.full(value.shape, 2.0**-32, F32)
    for step in (32, 16, 8, 4, 2, 1):
        more = power * 2.0**step
        power = jnp.where(power * 2.0 ** (step - 1) < value, more, power)
    return power


def slices(value, count):
    parts = []
    for k in range(count):
        step = 2.0 ** (8 + 9 * k)
        piece = jnp.round(value * step) * (1.0 / step)
        parts.append(piece.astype(jnp.bfloat16))
        value = value - piece
    return parts, value


def exact_dot(a, b):
    return lax.dot_general(
        a, b, (((1,), (0,)), ((), ())), preferred_element_type=F32
    )


def upper_half(square):
    row = lax.broadcasted_iota(jnp.int32, square.shape, 0)
    column = lax.broadcasted_iota(jnp.int32, square.shape, 1)
    return jnp.where(row < column, square, jnp.where(row == column, 0.5 * square, 0.0))


def split(value):
    one = value.astype(jnp.bfloat16)
    rest = value - one.astype(F32)
    two = rest.astype(jnp.bfloat16)
    return one, two, (rest - two.astype(F32)).astype(jnp.bfloat16)


def final_kernel(
    points, slices_in, gram, q_out, factor, block, state, back, result, load_sem, store_sem
):
    load = pltpu.make_async_copy(slices_in, block, load_sem)
    load.start()
    nx, rows, width = gram.shape[0], gram.shape[1] // 2 - 1, gram.shape[2]
    high, low = [
        unpacked(
            jnp.concatenate([gram[c, at : at + rows] for c in range(nx)], axis=0),
            gram[0, alone : alone + 1],
        )
        * (1.0 / points)
        for at, alone in ((0, 2 * rows), (rows, 2 * rows + 1))
    ]
    row = lax.broadcasted_iota(jnp.int32, high.shape, 0)
    column = lax.broadcasted_iota(jnp.int32, high.shape, 1)
    diagonal = jnp.where(row == column, high, 0.0)
    down = 1.0 / power_above(jnp.sqrt(jnp.sum(diagonal, axis=1, keepdims=True)))
    across = 1.0 / power_above(jnp.sqrt(jnp.sum(diagonal, axis=0, keepdims=True)))
    high = high * down * across
    low = low * down * across
    state[...] = high.reshape(state.shape)
    inverse_factor(state, back)
    lower = back[...].reshape(width, width)
    size = power_above(jnp.max(jnp.abs(lower), axis=1, keepdims=True))
    b, rest = slices(lower * (1.0 / size), 3)
    lower = lower - rest * size
    g, rest = slices(high, 3)
    g.append((rest + low).astype(jnp.bfloat16))
    image = exact_dot(b[0], g[0])
    image = image + (exact_dot(b[0], g[1]) + exact_dot(b[1], g[0]))
    image = image + (exact_dot(b[0], g[2]) + exact_dot(b[1], g[1]) + exact_dot(b[2], g[0]))
    image = image + (exact_dot(b[0], g[3]) + exact_dot(b[1], g[2]) + exact_dot(b[2], g[1]))
    image = image * size
    error = product(image, lower, ((1,), (1,))) - jnp.where(row == column, 1.0, 0.0)
    x = upper_half(error)
    for _ in range(2):
        x = upper_half(error - product(x, x, ((0,), (0,))))
    both = jnp.concatenate([lower, image], axis=1)
    x2 = product(x, x, ((1,), (0,)))
    both = both - product(x, both, ((0,), (0,)))
    both = both + product(x2, both, ((0,), (0,)))
    lower = both[:, :width] * across
    factor[...] = jnp.where(row <= column, both[:, width:] * (1.0 / across), 0.0)
    one, two, three = split(lower.T)
    both = jnp.concatenate([one, two], axis=1)
    both = jnp.concatenate([both, both], axis=0)
    ends = jnp.concatenate([three, one], axis=0)
    load.wait()

    def apply(x, carry):
        rows = block[x]
        q = exact_dot(rows[:, : 2 * width], both)
        small = exact_dot(jnp.concatenate([rows[:, :width], rows[:, 2 * width :]], axis=1), ends)
        q = q[:, :width] + (q[:, width:] + small)
        result[x] = q.reshape(result.shape[1:])
        pltpu.make_async_copy(result.at[x], q_out.at[x], store_sem.at[x]).start()
        return carry

    lax.fori_loop(0, block.shape[0], apply, 0)

    def drain(x, carry):
        pltpu.make_async_copy(result.at[x], q_out.at[x], store_sem.at[x]).wait()
        return carry

    lax.fori_loop(0, block.shape[0], drain, 0)


def local(sizes, orbitals_in, potential):
    bx, by, bz, width = orbitals_in.shape
    points = bx * by * bz * sizes[0] * sizes[1] * sizes[2]
    nx = sizes[0]
    rows = width // 2 // nx
    longest = max(sizes)
    vmem = pl.BlockSpec(memory_space=pltpu.VMEM)
    anywhere = pl.BlockSpec(memory_space=pl.ANY)
    chunk = (2 * rows + 2, width)
    chunks = jax.ShapeDtypeStruct((nx, *chunk), F32)
    slices_shape = jax.ShapeDtypeStruct((bx, by * bz, 3 * width), jnp.bfloat16)
    tiles = (width // 8, 8, width)
    square = jax.ShapeDtypeStruct((width, width), F32)
    pieces, gram = pl.pallas_call(
        functools.partial(filter_kernel, sizes),
        out_shape=(slices_shape, chunks),
        in_specs=[anywhere, anywhere],
        out_specs=(anywhere, vmem),
        scratch_shapes=[
            pltpu.VMEM((bx + 2, by + 2, bz, width), F32),
            pltpu.VMEM((bx + 2, by + 2, bz, width), F32),
            pltpu.VMEM((2, bx, by, width), F32),
            pltpu.VMEM((2, bx, by, width), F32),
            pltpu.VMEM((2, 2, bx, by, width), F32),
            pltpu.VMEM(slices_shape.shape, jnp.bfloat16),
            pltpu.VMEM((bx, by, bz), F32),
            pltpu.VMEM((bx, bz, by), F32),
            pltpu.VMEM((3, width, width), F32),
            pltpu.VMEM(chunks.shape, F32),
            pltpu.VMEM((3, *chunk), F32),
            pltpu.VMEM((3, longest, *chunk), F32),
            pltpu.SemaphoreType.DMA((2,)),
            pltpu.SemaphoreType.DMA(()),
            pltpu.SemaphoreType.DMA((2, 6)),
            pltpu.SemaphoreType.DMA((2, 6)),
            pltpu.SemaphoreType.DMA((4, longest)),
            pltpu.SemaphoreType.DMA((4, longest)),
        ],
        compiler_params=pltpu.CompilerParams(collective_id=0, has_side_effects=True),
        name="filter_gram",
    )(orbitals_in, potential)
    return pl.pallas_call(
        functools.partial(final_kernel, points),
        out_shape=(jax.ShapeDtypeStruct(orbitals_in.shape, F32), square),
        in_specs=[anywhere, vmem],
        out_specs=(anywhere, vmem),
        scratch_shapes=[
            pltpu.VMEM(slices_shape.shape, jnp.bfloat16),
            pltpu.VMEM(tiles, F32),
            pltpu.VMEM(tiles, F32),
            pltpu.VMEM(orbitals_in.shape, F32),
            pltpu.SemaphoreType.DMA(()),
            pltpu.SemaphoreType.DMA((bx,)),
        ],
        name="factor_apply",
    )(pieces, gram)


def solution(mesh):
    sizes = tuple(mesh.shape[a] for a in AXES)
    spec = P("gx", "gy", "gz", None)
    return jax.shard_map(
        functools.partial(local, sizes),
        mesh=mesh,
        in_specs=(spec, P("gx", "gy", "gz")),
        out_specs=(spec, P()),
        check_vma=False,
    )
```

```python
import functools

import jax
import jax.numpy as jnp
from jax import lax
from jax.experimental import pallas as pl
from jax.experimental.pallas import tpu as pltpu
from jax.sharding import PartitionSpec as P

AXES = ("gx", "gy", "gz")
HIGHEST = lax.Precision.HIGHEST
F32 = jnp.float32
MESH = pl.DeviceIdType.MESH


def position():
    return tuple(lax.axis_index(a) for a in AXES)


def moved(place, dim, index):
    return tuple(index if d == dim else place[d] for d in range(3))


def greet(place, sizes):
    barrier = pltpu.get_barrier_semaphore()
    for dim in range(3):
        for off in range(1, sizes[dim]):
            peer = lax.rem(place[dim] + off, sizes[dim])
            pl.semaphore_signal(
                barrier, inc=1, device_id=moved(place, dim, peer), device_id_type=MESH
            )
    return lambda: pl.semaphore_wait(barrier, sum(n - 1 for n in sizes))


def line_copies(source, target, place, dim, size, send, recv):
    copies = []
    for off in range(1, size):
        peer = lax.rem(place[dim] + off, size)
        copies.append(
            pltpu.make_async_remote_copy(
                src_ref=source(peer),
                dst_ref=target,
                send_sem=send.at[off],
                recv_sem=recv.at[off],
                device_id=moved(place, dim, peer),
                device_id_type=MESH,
            )
        )
    for copy in copies:
        copy.start()
    return copies


def two_sum(a, b):
    total = a + b
    back = total - a
    return total, (a - (total - back)) + (b - back)


def pair_add(high, low, other_high, other_low):
    high, error = two_sum(high, other_high)
    return high, low + (error + other_low)


def packed(square):
    half = square.shape[0] // 2
    top, bottom = square[:half], square[half:]
    row = lax.broadcasted_iota(jnp.int32, top.shape, 0)
    lane = lax.broadcasted_iota(jnp.int32, top.shape, 1)
    rest = jnp.sum(jnp.where(lane == row + half, bottom, 0.0), axis=0, keepdims=True)
    return jnp.where(lane < row, pltpu.roll(bottom, half, 1), top), rest


def unpacked(rows, rest):
    half, width = rows.shape
    both = jnp.concatenate([rows, pltpu.roll(rows, half, 1)], axis=0)
    turned = both.T
    row = lax.broadcasted_iota(jnp.int32, both.shape, 0)
    lane = lax.broadcasted_iota(jnp.int32, both.shape, 1)
    take = ((row < half) & (lane >= row)) | ((row >= half) & (lane >= half) & (lane < row))
    full = jnp.where(take, both, turned)
    return jnp.where((row >= half) & (lane == row), jnp.broadcast_to(rest, both.shape), full)


def sum_slots(slots, count, rows):
    pairs = []
    for high_at, low_at in (
        (pl.ds(0, rows), pl.ds(rows, rows)),
        (pl.ds(2 * rows, 1), pl.ds(2 * rows + 1, 1)),
    ):
        high, low = slots[0, high_at], slots[0, low_at]
        for other in range(1, count):
            high, low = pair_add(high, low, slots[other, high_at], slots[other, low_at])
        pairs += [(high_at, high), (low_at, low)]
    return pairs


def all_reduce(gram, out, place, sizes, part, land, send, recv):
    nx, ny, nz = sizes
    me = place[0]
    rows = gram.shape[1] // 2 - 1
    copies = line_copies(
        lambda peer: gram.at[peer], land.at[0, me], place, 0, nx, send.at[0], recv.at[0]
    )
    land[0, me] = gram[me]
    for stage in range(3):
        for copy in copies:
            copy.wait()
        pairs = sum_slots(land.at[stage], sizes[stage], rows)
        if stage == 2:
            break
        dim = stage + 1
        for target in (part.at[stage], land.at[dim, place[dim]]):
            for at, value in pairs:
                target[at] = value
        copies = line_copies(
            lambda peer: part.at[stage],
            land.at[dim, place[dim]],
            place,
            dim,
            sizes[dim],
            send.at[dim],
            recv.at[dim],
        )
    for target in (part.at[2], out.at[me]):
        for at, value in pairs:
            target[at] = value
    copies = line_copies(
        lambda peer: part.at[2], out.at[me], place, 0, nx, send.at[3], recv.at[3]
    )
    for copy in copies:
        copy.wait()


def halo_exchange(source, first, field, low_z, high_z, faces, place, sizes, block, send, recv, pack):
    bx, by, bz = block
    inner_x, inner_y = pl.ds(1, bx), pl.ds(1, by)
    from_x, from_y = pl.ds(first, bx), pl.ds(first, by)
    moves = (
        (0, -1, source.at[first, from_y], field.at[bx + 1, inner_y]),
        (0, 1, source.at[first + bx - 1, from_y], field.at[0, inner_y]),
        (1, -1, source.at[from_x, first], field.at[inner_x, by + 1]),
        (1, 1, source.at[from_x, first + by - 1], field.at[inner_x, 0]),
        (2, -1, faces.at[0], high_z),
        (2, 1, faces.at[1], low_z),
    )
    pairs = []
    for number, (dim, step, source, target) in enumerate(moves):
        index = place[dim]
        sends = index > 0 if step < 0 else index < sizes[dim] - 1
        gets = index < sizes[dim] - 1 if step < 0 else index > 0
        peer = lax.rem(index + step + sizes[dim], sizes[dim])
        copy = pltpu.make_async_remote_copy(
            src_ref=source,
            dst_ref=target,
            send_sem=send.at[number],
            recv_sem=recv.at[number],
            device_id=moved(place, dim, peer),
            device_id_type=MESH,
        )
        pairs.append((sends, gets, copy, target))
    for sends, gets, copy, target in pairs[:4]:
        pl.when(sends)(copy.start)
    pack()
    for sends, gets, copy, target in pairs[4:]:
        pl.when(sends)(copy.start)
    for sends, gets, copy, target in pairs:

        @pl.when(jnp.logical_not(gets))
        def _():
            target[...] = jnp.zeros(target.shape, F32)

    def finish():
        for sends, gets, copy, target in pairs:
            pl.when(gets)(copy.wait_recv)
            pl.when(sends)(copy.wait_send)

    return finish


def pack_faces(field, faces, block):
    bx, by, bz = block

    def one(x, carry):
        faces[0, x] = field[x + 1, pl.ds(1, by), 0, :]
        faces[1, x] = field[x + 1, pl.ds(1, by), bz - 1, :]
        return carry

    lax.fori_loop(0, bx, one, 0, unroll=4)


def neighbour_sums(field, low_z, high_z, x, y, sub, bz):
    centre = field[x + 1, y + 1]
    beside = field[x, y + 1] + field[x + 2, y + 1]
    beside = beside + (field[x + 1, y] + field[x + 1, y + 2])
    below = jnp.where(sub == 0, low_z[x, pl.ds(y, 1), :], pltpu.roll(centre, 1, 0))
    above = jnp.where(
        sub == bz - 1, high_z[x, pl.ds(y, 1), :], pltpu.roll(centre, bz - 1, 0)
    )
    return centre, beside + (below + above)


def add_gram(sums, rows, pieces):
    width = rows.shape[1]
    one = rows.astype(jnp.bfloat16)
    rest = rows - one.astype(F32)
    two = rest.astype(jnp.bfloat16)
    three = (rest - two.astype(F32)).astype(jnp.bfloat16)
    for k, piece in enumerate((one, two, three)):
        pieces[:, k * width : (k + 1) * width] = piece
    dims = (((0,), (0,)), ((), ()))
    first = lax.dot_general(
        one, jnp.concatenate([one, two, three], axis=1), dims, preferred_element_type=F32
    )
    later = lax.dot_general(
        two, jnp.concatenate([two, three], axis=1), dims, preferred_element_type=F32
    )
    squares = jnp.sum(rows * rows, axis=0, keepdims=True)
    row = lax.broadcasted_iota(jnp.int32, (width, width), 0)
    lane = lax.broadcasted_iota(jnp.int32, (width, width), 1)
    top = jnp.where(row == lane, jnp.broadcast_to(squares, row.shape), first[:, :width])
    high, error = two_sum(sums[0], top)
    sums[0] = high
    sums[1] = sums[1] + error
    small = first[:, 2 * width :] + later[:, width:] + 0.5 * later[:, :width]
    sums[2] = sums[2] + (first[:, width : 2 * width] + small)


def filter_kernel(
    sizes, orb, pot_in, slices_out, gram_out,
    field, middle, low_z, high_z, faces, pieces, pot, turned, sums, gram, part, land,
    load_sem, store_sem, halo_send, halo_recv, line_send, line_recv,
):
    place = position()
    bx, by, bz, width = orb.shape
    block = (bx, by, bz)
    met = greet(place, sizes)
    load = pltpu.make_async_copy(orb, field.at[pl.ds(1, bx), pl.ds(1, by)], load_sem.at[0])
    load.start()
    load_pot = pltpu.make_async_copy(pot_in, pot, load_sem.at[1])
    load_pot.start()
    met()

    def pack_first():
        load.wait()
        pack_faces(field, faces.at[0], block)

    finish = halo_exchange(
        orb, 0, field, low_z.at[0], high_z.at[0], faces.at[0], place, sizes, block,
        halo_send.at[0], halo_recv.at[0], pack_first,
    )
    load_pot.wait()

    def turn(x, carry):
        turned[x] = pot[x].T
        return carry

    lax.fori_loop(0, bx, turn, 0)
    finish()
    sub = lax.broadcasted_iota(jnp.int32, (bz, width), 0)

    def first(x, carry):
        scale = 0.2 * turned[x] - 0.4
        for y in range(by):
            centre, beside = neighbour_sums(field, low_z.at[0], high_z.at[0], x, y, sub, bz)
            middle[x + 1, y + 1] = scale[:, y : y + 1] * centre - 0.1 * beside
        return carry

    lax.fori_loop(0, bx, first, 0, unroll=2)
    finish = halo_exchange(
        middle, 1, middle, low_z.at[1], high_z.at[1], faces.at[1], place, sizes, block,
        halo_send.at[1], halo_recv.at[1], lambda: pack_faces(middle, faces.at[1], block),
    )
    sums[...] = jnp.zeros(sums.shape, F32)
    finish()

    def second(x, carry):
        scale = 0.4 * turned[x] - 0.8
        lines = []
        for y in range(by):
            centre, beside = neighbour_sums(middle, low_z.at[1], high_z.at[1], x, y, sub, bz)
            lines.append(scale[:, y : y + 1] * centre - 0.2 * beside - field[x + 1, y + 1])
        add_gram(sums, jnp.concatenate(lines, axis=0), pieces.at[x])
        return carry

    lax.fori_loop(0, bx, second, 0, unroll=2)
    store = pltpu.make_async_copy(pieces, slices_out, store_sem)
    store.start()
    row = lax.broadcasted_iota(jnp.int32, (width, width), 0)
    lane = lax.broadcasted_iota(jnp.int32, (width, width), 1)
    cross = jnp.where(row == lane, 0.0, sums[2])
    high, low = two_sum(sums[0], sums[1] + (cross + cross.T))
    rows = gram.shape[1] // 2 - 1
    for value, at, alone in ((high, 0, 2 * rows), (low, rows, 2 * rows + 1)):
        value, rest = packed(value)
        for chunk in range(gram.shape[0]):
            gram[chunk, at : at + rows] = value[chunk * rows : (chunk + 1) * rows]
            gram[chunk, alone : alone + 1] = rest
    all_reduce(gram, gram_out, place, sizes, part, land, line_send, line_recv)
    store.wait()


def spread(row, height=8):
    return jnp.broadcast_to(row, (height, row.shape[1]))


def inverse_factor(state, result):
    tiles, high, wide = state.shape
    lane = lax.broadcasted_iota(jnp.int32, (high, wide), 1)
    row = lax.broadcasted_iota(jnp.int32, (high, wide), 0)
    for p in range(tiles):
        j0 = p * high
        inside = (lane >= j0) & (lane < j0 + high)
        panel = state[p]
        columns = [jnp.broadcast_to(panel[:, j0 + t : j0 + t + 1], (high, wide)) for t in range(high)]
        d = [[spread(columns[t][i : i + 1]) if i >= t else None for t in range(high)] for i in range(high)]
        line = jnp.where(inside, jnp.where(lane - j0 == row, 1.0, 0.0), panel)
        lines = [spread(line[t : t + 1]) for t in range(high)]
        below = []
        for i in range(p + 1, tiles):
            other = state[i]
            parts = [
                jnp.broadcast_to(other[:, j0 + t : j0 + t + 1], (high, wide))
                for t in range(high)
            ]
            below.append([i, jnp.where(inside, 0.0, other), parts])
        block = None
        for t in range(high):
            rec = 1.0 / d[t][t]
            for i in range(t + 1, high):
                m = d[i][t] * rec
                for u in range(t + 1, i + 1):
                    d[i][u] = d[i][u] - m * d[u][t]
                lines[i] = lines[i] - m * lines[t]
            for entry in below:
                parts = entry[2]
                m = parts[t] * rec
                for u in range(t + 1, high):
                    parts[u] = parts[u] - m * d[u][t]
                entry[1] = entry[1] - m * lines[t]
            scaled = lines[t] * lax.rsqrt(d[t][t])
            block = scaled if block is None else jnp.where(row == t, scaled, block)
        for i, value, _ in below:
            state[i] = value
        result[p] = jnp.where(lane <= j0 + row, block, 0.0)


def product(a, b, dims):
    return lax.dot_general(
        a, b, (dims, ((), ())), precision=HIGHEST, preferred_element_type=F32
    )


def power_above(value):
    power = jnp.full(value.shape, 2.0**-32, F32)
    for step in (32, 16, 8, 4, 2, 1):
        more = power * 2.0**step
        power = jnp.where(power * 2.0 ** (step - 1) < value, more, power)
    return power


def slices(value, count):
    parts = []
    for k in range(count):
        step = 2.0 ** (8 + 9 * k)
        piece = jnp.round(value * step) * (1.0 / step)
        parts.append(piece.astype(jnp.bfloat16))
        value = value - piece
    return parts, value


def exact_dot(a, b):
    return lax.dot_general(
        a, b, (((1,), (0,)), ((), ())), preferred_element_type=F32
    )


def upper_half(square):
    row = lax.broadcasted_iota(jnp.int32, square.shape, 0)
    column = lax.broadcasted_iota(jnp.int32, square.shape, 1)
    return jnp.where(row < column, square, jnp.where(row == column, 0.5 * square, 0.0))


def split(value):
    one = value.astype(jnp.bfloat16)
    rest = value - one.astype(F32)
    two = rest.astype(jnp.bfloat16)
    return one, two, (rest - two.astype(F32)).astype(jnp.bfloat16)


def final_kernel(
    points, slices_in, gram, q_out, factor, block, state, back, result, load_sem, store_sem
):
    load = pltpu.make_async_copy(slices_in, block, load_sem)
    load.start()
    nx, rows, width = gram.shape[0], gram.shape[1] // 2 - 1, gram.shape[2]
    high, low = [
        unpacked(
            jnp.concatenate([gram[c, at : at + rows] for c in range(nx)], axis=0),
            gram[0, alone : alone + 1],
        )
        * (1.0 / points)
        for at, alone in ((0, 2 * rows), (rows, 2 * rows + 1))
    ]
    row = lax.broadcasted_iota(jnp.int32, high.shape, 0)
    column = lax.broadcasted_iota(jnp.int32, high.shape, 1)
    diagonal = jnp.where(row == column, high, 0.0)
    down = 1.0 / power_above(jnp.sqrt(jnp.sum(diagonal, axis=1, keepdims=True)))
    across = 1.0 / power_above(jnp.sqrt(jnp.sum(diagonal, axis=0, keepdims=True)))
    high = high * down * across
    low = low * down * across
    state[...] = high.reshape(state.shape)
    inverse_factor(state, back)
    lower = back[...].reshape(width, width)
    size = power_above(jnp.max(jnp.abs(lower), axis=1, keepdims=True))
    b, rest = slices(lower * (1.0 / size), 3)
    lower = lower - rest * size
    g, rest = slices(high, 3)
    g.append((rest + low).astype(jnp.bfloat16))
    image = exact_dot(b[0], g[0])
    image = image + (exact_dot(b[0], g[1]) + exact_dot(b[1], g[0]))
    image = image + (exact_dot(b[0], g[2]) + exact_dot(b[1], g[1]) + exact_dot(b[2], g[0]))
    image = image + (exact_dot(b[0], g[3]) + exact_dot(b[1], g[2]) + exact_dot(b[2], g[1]))
    image = image * size
    error = product(image, lower, ((1,), (1,))) - jnp.where(row == column, 1.0, 0.0)
    x = upper_half(error)
    for _ in range(2):
        x = upper_half(error - product(x, x, ((0,), (0,))))
    both = jnp.concatenate([lower, image], axis=1)
    x2 = product(x, x, ((1,), (0,)))
    both = both - product(x, both, ((0,), (0,)))
    both = both + product(x2, both, ((0,), (0,)))
    lower = both[:, :width] * across
    factor[...] = jnp.where(row <= column, both[:, width:] * (1.0 / across), 0.0)
    one, two, three = split(lower.T)
    both = jnp.concatenate([one, two], axis=1)
    both = jnp.concatenate([both, both], axis=0)
    ends = jnp.concatenate([three, one], axis=0)
    load.wait()

    def apply(x, carry):
        rows = block[x]
        q = exact_dot(rows[:, : 2 * width], both)
        small = exact_dot(jnp.concatenate([rows[:, :width], rows[:, 2 * width :]], axis=1), ends)
        q = q[:, :width] + (q[:, width:] + small)
        result[x] = q.reshape(result.shape[1:])
        pltpu.make_async_copy(result.at[x], q_out.at[x], store_sem.at[x]).start()
        return carry

    lax.fori_loop(0, block.shape[0], apply, 0, unroll=True)

    def drain(x, carry):
        pltpu.make_async_copy(result.at[x], q_out.at[x], store_sem.at[x]).wait()
        return carry

    lax.fori_loop(0, block.shape[0], drain, 0)


def local(sizes, orbitals_in, potential):
    bx, by, bz, width = orbitals_in.shape
    points = bx * by * bz * sizes[0] * sizes[1] * sizes[2]
    nx = sizes[0]
    rows = width // 2 // nx
    longest = max(sizes)
    vmem = pl.BlockSpec(memory_space=pltpu.VMEM)
    anywhere = pl.BlockSpec(memory_space=pl.ANY)
    chunk = (2 * rows + 2, width)
    chunks = jax.ShapeDtypeStruct((nx, *chunk), F32)
    slices_shape = jax.ShapeDtypeStruct((bx, by * bz, 3 * width), jnp.bfloat16)
    tiles = (width // 8, 8, width)
    square = jax.ShapeDtypeStruct((width, width), F32)
    pieces, gram = pl.pallas_call(
        functools.partial(filter_kernel, sizes),
        out_shape=(slices_shape, chunks),
        in_specs=[anywhere, anywhere],
        out_specs=(anywhere, vmem),
        scratch_shapes=[
            pltpu.VMEM((bx + 2, by + 2, bz, width), F32),
            pltpu.VMEM((bx + 2, by + 2, bz, width), F32),
            pltpu.VMEM((2, bx, by, width), F32),
            pltpu.VMEM((2, bx, by, width), F32),
            pltpu.VMEM((2, 2, bx, by, width), F32),
            pltpu.VMEM(slices_shape.shape, jnp.bfloat16),
            pltpu.VMEM((bx, by, bz), F32),
            pltpu.VMEM((bx, bz, by), F32),
            pltpu.VMEM((3, width, width), F32),
            pltpu.VMEM(chunks.shape, F32),
            pltpu.VMEM((3, *chunk), F32),
            pltpu.VMEM((3, longest, *chunk), F32),
            pltpu.SemaphoreType.DMA((2,)),
            pltpu.SemaphoreType.DMA(()),
            pltpu.SemaphoreType.DMA((2, 6)),
            pltpu.SemaphoreType.DMA((2, 6)),
            pltpu.SemaphoreType.DMA((4, longest)),
            pltpu.SemaphoreType.DMA((4, longest)),
        ],
        compiler_params=pltpu.CompilerParams(collective_id=0, has_side_effects=True),
        name="filter_gram",
    )(orbitals_in, potential)
    return pl.pallas_call(
        functools.partial(final_kernel, points),
        out_shape=(jax.ShapeDtypeStruct(orbitals_in.shape, F32), square),
        in_specs=[anywhere, vmem],
        out_specs=(anywhere, vmem),
        scratch_shapes=[
            pltpu.VMEM(slices_shape.shape, jnp.bfloat16),
            pltpu.VMEM(tiles, F32),
            pltpu.VMEM(tiles, F32),
            pltpu.VMEM(orbitals_in.shape, F32),
            pltpu.SemaphoreType.DMA(()),
            pltpu.SemaphoreType.DMA((bx,)),
        ],
        name="factor_apply",
    )(pieces, gram)


def solution(mesh):
    sizes = tuple(mesh.shape[a] for a in AXES)
    spec = P("gx", "gy", "gz", None)
    return jax.shard_map(
        functools.partial(local, sizes),
        mesh=mesh,
        in_specs=(spec, P("gx", "gy", "gz")),
        out_specs=(spec, P()),
        check_vma=False,
    )
```

```python
import functools

import jax
import jax.numpy as jnp
from jax import lax
from jax.experimental import pallas as pl
from jax.experimental.pallas import tpu as pltpu
from jax.sharding import PartitionSpec as P

AXES = ("gx", "gy", "gz")
HIGHEST = lax.Precision.HIGHEST
F32 = jnp.float32
MESH = pl.DeviceIdType.MESH


def position():
    return tuple(lax.axis_index(a) for a in AXES)


def moved(place, dim, index):
    return tuple(index if d == dim else place[d] for d in range(3))


def greet(place, sizes):
    barrier = pltpu.get_barrier_semaphore()
    for dim in range(3):
        for off in farthest_first(sizes[dim]):
            peer = lax.rem(place[dim] + off, sizes[dim])
            pl.semaphore_signal(
                barrier, inc=1, device_id=moved(place, dim, peer), device_id_type=MESH
            )
    return lambda: pl.semaphore_wait(barrier, sum(n - 1 for n in sizes))


def farthest_first(size):
    return sorted(range(1, size), key=lambda off: -min(off, size - off))


def line_copies(source, target, place, dim, size, send, recv):
    copies = []
    for off in farthest_first(size):
        peer = lax.rem(place[dim] + off, size)
        copies.append(
            pltpu.make_async_remote_copy(
                src_ref=source(peer),
                dst_ref=target,
                send_sem=send.at[off],
                recv_sem=recv.at[off],
                device_id=moved(place, dim, peer),
                device_id_type=MESH,
            )
        )
    for copy in copies:
        copy.start()
    return copies


def two_sum(a, b):
    total = a + b
    back = total - a
    return total, (a - (total - back)) + (b - back)


def pair_add(high, low, other_high, other_low):
    high, error = two_sum(high, other_high)
    return high, low + (error + other_low)


def packed(square):
    half = square.shape[0] // 2
    top, bottom = square[:half], square[half:]
    row = lax.broadcasted_iota(jnp.int32, top.shape, 0)
    lane = lax.broadcasted_iota(jnp.int32, top.shape, 1)
    rest = jnp.sum(jnp.where(lane == row + half, bottom, 0.0), axis=0, keepdims=True)
    return jnp.where(lane < row, pltpu.roll(bottom, half, 1), top), rest


def unpacked(rows, rest):
    half, width = rows.shape
    both = jnp.concatenate([rows, pltpu.roll(rows, half, 1)], axis=0)
    turned = both.T
    row = lax.broadcasted_iota(jnp.int32, both.shape, 0)
    lane = lax.broadcasted_iota(jnp.int32, both.shape, 1)
    take = ((row < half) & (lane >= row)) | ((row >= half) & (lane >= half) & (lane < row))
    full = jnp.where(take, both, turned)
    return jnp.where((row >= half) & (lane == row), jnp.broadcast_to(rest, both.shape), full)


def sum_slots(slots, count, rows):
    pairs = []
    for high_at, low_at in (
        (pl.ds(0, rows), pl.ds(rows, rows)),
        (pl.ds(2 * rows, 1), pl.ds(2 * rows + 1, 1)),
    ):
        high, low = slots[0, high_at], slots[0, low_at]
        for other in range(1, count):
            high, low = pair_add(high, low, slots[other, high_at], slots[other, low_at])
        pairs += [(high_at, high), (low_at, low)]
    return pairs


def all_reduce(gram, out, place, sizes, part, land, send, recv):
    nx, ny, nz = sizes
    me = place[0]
    rows = gram.shape[1] // 2 - 1
    copies = line_copies(
        lambda peer: gram.at[peer], land.at[0, me], place, 0, nx, send.at[0], recv.at[0]
    )
    land[0, me] = gram[me]
    for stage in range(3):
        for copy in copies:
            copy.wait()
        pairs = sum_slots(land.at[stage], sizes[stage], rows)
        if stage == 2:
            break
        dim = stage + 1
        for target in (part.at[stage], land.at[dim, place[dim]]):
            for at, value in pairs:
                target[at] = value
        copies = line_copies(
            lambda peer: part.at[stage],
            land.at[dim, place[dim]],
            place,
            dim,
            sizes[dim],
            send.at[dim],
            recv.at[dim],
        )
    for target in (part.at[2], out.at[me]):
        for at, value in pairs:
            target[at] = value
    copies = line_copies(
        lambda peer: part.at[2], out.at[me], place, 0, nx, send.at[3], recv.at[3]
    )
    for copy in copies:
        copy.wait()


def halo_exchange(source, first, field, low_z, high_z, faces, place, sizes, block, send, recv, pack):
    bx, by, bz = block
    inner_x, inner_y = pl.ds(1, bx), pl.ds(1, by)
    from_x, from_y = pl.ds(first, bx), pl.ds(first, by)
    moves = (
        (0, -1, source.at[first, from_y], field.at[bx + 1, inner_y]),
        (0, 1, source.at[first + bx - 1, from_y], field.at[0, inner_y]),
        (1, -1, source.at[from_x, first], field.at[inner_x, by + 1]),
        (1, 1, source.at[from_x, first + by - 1], field.at[inner_x, 0]),
        (2, -1, faces.at[0], high_z),
        (2, 1, faces.at[1], low_z),
    )
    pairs = []
    for number, (dim, step, source, target) in enumerate(moves):
        index = place[dim]
        sends = index > 0 if step < 0 else index < sizes[dim] - 1
        gets = index < sizes[dim] - 1 if step < 0 else index > 0
        peer = lax.rem(index + step + sizes[dim], sizes[dim])
        copy = pltpu.make_async_remote_copy(
            src_ref=source,
            dst_ref=target,
            send_sem=send.at[number],
            recv_sem=recv.at[number],
            device_id=moved(place, dim, peer),
            device_id_type=MESH,
        )
        pairs.append((sends, gets, copy, target))
    for sends, gets, copy, target in pairs[:4]:
        pl.when(sends)(copy.start)
    pack()
    for sends, gets, copy, target in pairs[4:]:
        pl.when(sends)(copy.start)
    for sends, gets, copy, target in pairs:

        @pl.when(jnp.logical_not(gets))
        def _():
            target[...] = jnp.zeros(target.shape, F32)

    def finish():
        for sends, gets, copy, target in pairs:
            pl.when(gets)(copy.wait_recv)
            pl.when(sends)(copy.wait_send)

    return finish


def pack_faces(field, faces, block):
    bx, by, bz = block

    def one(x, carry):
        faces[0, x] = field[x + 1, pl.ds(1, by), 0, :]
        faces[1, x] = field[x + 1, pl.ds(1, by), bz - 1, :]
        return carry

    lax.fori_loop(0, bx, one, 0, unroll=4)


def neighbour_sums(field, low_z, high_z, x, y, sub, bz):
    centre = field[x + 1, y + 1]
    beside = field[x, y + 1] + field[x + 2, y + 1]
    beside = beside + (field[x + 1, y] + field[x + 1, y + 2])
    below = jnp.where(sub == 0, low_z[x, pl.ds(y, 1), :], pltpu.roll(centre, 1, 0))
    above = jnp.where(
        sub == bz - 1, high_z[x, pl.ds(y, 1), :], pltpu.roll(centre, bz - 1, 0)
    )
    return centre, beside + (below + above)


def add_gram(sums, rows, pieces):
    width = rows.shape[1]
    one = rows.astype(jnp.bfloat16)
    rest = rows - one.astype(F32)
    two = rest.astype(jnp.bfloat16)
    three = (rest - two.astype(F32)).astype(jnp.bfloat16)
    for k, piece in enumerate((one, two, three)):
        pieces[:, k * width : (k + 1) * width] = piece
    dims = (((0,), (0,)), ((), ()))
    first = lax.dot_general(
        one, jnp.concatenate([one, two, three], axis=1), dims, preferred_element_type=F32
    )
    later = lax.dot_general(
        two, jnp.concatenate([two, three], axis=1), dims, preferred_element_type=F32
    )
    squares = jnp.sum(rows * rows, axis=0, keepdims=True)
    row = lax.broadcasted_iota(jnp.int32, (width, width), 0)
    lane = lax.broadcasted_iota(jnp.int32, (width, width), 1)
    top = jnp.where(row == lane, jnp.broadcast_to(squares, row.shape), first[:, :width])
    high, error = two_sum(sums[0], top)
    sums[0] = high
    sums[1] = sums[1] + error
    small = first[:, 2 * width :] + later[:, width:] + 0.5 * later[:, :width]
    sums[2] = sums[2] + (first[:, width : 2 * width] + small)


def filter_kernel(
    sizes, orb, pot_in, slices_out, gram_out,
    field, middle, low_z, high_z, faces, pieces, pot, turned, sums, gram, part, land,
    load_sem, store_sem, halo_send, halo_recv, line_send, line_recv,
):
    place = position()
    bx, by, bz, width = orb.shape
    block = (bx, by, bz)
    met = greet(place, sizes)
    load = pltpu.make_async_copy(orb, field.at[pl.ds(1, bx), pl.ds(1, by)], load_sem.at[0])
    load.start()
    load_pot = pltpu.make_async_copy(pot_in, pot, load_sem.at[1])
    load_pot.start()
    met()

    def pack_first():
        load.wait()
        pack_faces(field, faces.at[0], block)

    finish = halo_exchange(
        orb, 0, field, low_z.at[0], high_z.at[0], faces.at[0], place, sizes, block,
        halo_send.at[0], halo_recv.at[0], pack_first,
    )
    load_pot.wait()

    def turn(x, carry):
        turned[x] = pot[x].T
        return carry

    lax.fori_loop(0, bx, turn, 0)
    finish()
    sub = lax.broadcasted_iota(jnp.int32, (bz, width), 0)

    def first(x, carry):
        scale = 0.2 * turned[x] - 0.4
        for y in range(by):
            centre, beside = neighbour_sums(field, low_z.at[0], high_z.at[0], x, y, sub, bz)
            middle[x + 1, y + 1] = scale[:, y : y + 1] * centre - 0.1 * beside
        return carry

    lax.fori_loop(0, bx, first, 0, unroll=4)
    finish = halo_exchange(
        middle, 1, middle, low_z.at[1], high_z.at[1], faces.at[1], place, sizes, block,
        halo_send.at[1], halo_recv.at[1], lambda: pack_faces(middle, faces.at[1], block),
    )
    sums[...] = jnp.zeros(sums.shape, F32)
    finish()

    def second(x, carry):
        scale = 0.4 * turned[x] - 0.8
        lines = []
        for y in range(by):
            centre, beside = neighbour_sums(middle, low_z.at[1], high_z.at[1], x, y, sub, bz)
            lines.append(scale[:, y : y + 1] * centre - 0.2 * beside - field[x + 1, y + 1])
        add_gram(sums, jnp.concatenate(lines, axis=0), pieces.at[x])
        return carry

    lax.fori_loop(0, bx, second, 0, unroll=4)
    store = pltpu.make_async_copy(pieces, slices_out, store_sem)
    store.start()
    row = lax.broadcasted_iota(jnp.int32, (width, width), 0)
    lane = lax.broadcasted_iota(jnp.int32, (width, width), 1)
    cross = jnp.where(row == lane, 0.0, sums[2])
    high, low = two_sum(sums[0], sums[1] + (cross + cross.T))
    rows = gram.shape[1] // 2 - 1
    for value, at, alone in ((high, 0, 2 * rows), (low, rows, 2 * rows + 1)):
        value, rest = packed(value)
        for chunk in range(gram.shape[0]):
            gram[chunk, at : at + rows] = value[chunk * rows : (chunk + 1) * rows]
            gram[chunk, alone : alone + 1] = rest
    all_reduce(gram, gram_out, place, sizes, part, land, line_send, line_recv)
    store.wait()


def spread(row, height=8):
    return jnp.broadcast_to(row, (height, row.shape[1]))


def inverse_factor(state, result):
    tiles, high, wide = state.shape
    lane = lax.broadcasted_iota(jnp.int32, (high, wide), 1)
    row = lax.broadcasted_iota(jnp.int32, (high, wide), 0)
    for p in range(tiles):
        j0 = p * high
        inside = (lane >= j0) & (lane < j0 + high)
        panel = state[p]
        columns = [jnp.broadcast_to(panel[:, j0 + t : j0 + t + 1], (high, wide)) for t in range(high)]
        d = [[spread(columns[t][i : i + 1]) if i >= t else None for t in range(high)] for i in range(high)]
        line = jnp.where(inside, jnp.where(lane - j0 == row, 1.0, 0.0), panel)
        lines = [spread(line[t : t + 1]) for t in range(high)]
        below = []
        for i in range(p + 1, tiles):
            other = state[i]
            parts = [
                jnp.broadcast_to(other[:, j0 + t : j0 + t + 1], (high, wide))
                for t in range(high)
            ]
            below.append([i, jnp.where(inside, 0.0, other), parts])
        block = None
        for t in range(high):
            rec = 1.0 / d[t][t]
            for i in range(t + 1, high):
                m = d[i][t] * rec
                for u in range(t + 1, i + 1):
                    d[i][u] = d[i][u] - m * d[u][t]
                lines[i] = lines[i] - m * lines[t]
            for entry in below:
                parts = entry[2]
                m = parts[t] * rec
                for u in range(t + 1, high):
                    parts[u] = parts[u] - m * d[u][t]
                entry[1] = entry[1] - m * lines[t]
            scaled = lines[t] * lax.rsqrt(d[t][t])
            block = scaled if block is None else jnp.where(row == t, scaled, block)
        for i, value, _ in below:
            state[i] = value
        result[p] = jnp.where(lane <= j0 + row, block, 0.0)


def product(a, b, dims):
    return lax.dot_general(
        a, b, (dims, ((), ())), precision=HIGHEST, preferred_element_type=F32
    )


def power_above(value):
    power = jnp.full(value.shape, 2.0**-32, F32)
    for step in (32, 16, 8, 4, 2, 1):
        more = power * 2.0**step
        power = jnp.where(power * 2.0 ** (step - 1) < value, more, power)
    return power


def slices(value, count):
    parts = []
    for k in range(count):
        step = 2.0 ** (8 + 9 * k)
        piece = jnp.round(value * step) * (1.0 / step)
        parts.append(piece.astype(jnp.bfloat16))
        value = value - piece
    return parts, value


def exact_dot(a, b):
    return lax.dot_general(
        a, b, (((1,), (0,)), ((), ())), preferred_element_type=F32
    )


def upper_half(square):
    row = lax.broadcasted_iota(jnp.int32, square.shape, 0)
    column = lax.broadcasted_iota(jnp.int32, square.shape, 1)
    return jnp.where(row < column, square, jnp.where(row == column, 0.5 * square, 0.0))


def split(value):
    one = value.astype(jnp.bfloat16)
    rest = value - one.astype(F32)
    two = rest.astype(jnp.bfloat16)
    return one, two, (rest - two.astype(F32)).astype(jnp.bfloat16)


def final_kernel(
    points, slices_in, gram, q_out, factor, block, state, back, result, load_sem, store_sem
):
    load = pltpu.make_async_copy(slices_in, block, load_sem)
    load.start()
    nx, rows, width = gram.shape[0], gram.shape[1] // 2 - 1, gram.shape[2]
    high, low = [
        unpacked(
            jnp.concatenate([gram[c, at : at + rows] for c in range(nx)], axis=0),
            gram[0, alone : alone + 1],
        )
        * (1.0 / points)
        for at, alone in ((0, 2 * rows), (rows, 2 * rows + 1))
    ]
    row = lax.broadcasted_iota(jnp.int32, high.shape, 0)
    column = lax.broadcasted_iota(jnp.int32, high.shape, 1)
    diagonal = jnp.where(row == column, high, 0.0)
    down = 1.0 / power_above(jnp.sqrt(jnp.sum(diagonal, axis=1, keepdims=True)))
    across = 1.0 / power_above(jnp.sqrt(jnp.sum(diagonal, axis=0, keepdims=True)))
    high = high * down * across
    low = low * down * across
    state[...] = high.reshape(state.shape)
    inverse_factor(state, back)
    lower = back[...].reshape(width, width)
    size = power_above(jnp.max(jnp.abs(lower), axis=1, keepdims=True))
    b, rest = slices(lower * (1.0 / size), 3)
    lower = lower - rest * size
    g, rest = slices(high, 3)
    g.append((rest + low).astype(jnp.bfloat16))
    image = exact_dot(b[0], g[0])
    image = image + (exact_dot(b[0], g[1]) + exact_dot(b[1], g[0]))
    image = image + (exact_dot(b[0], g[2]) + exact_dot(b[1], g[1]) + exact_dot(b[2], g[0]))
    image = image + (exact_dot(b[0], g[3]) + exact_dot(b[1], g[2]) + exact_dot(b[2], g[1]))
    image = image * size
    error = product(image, lower, ((1,), (1,))) - jnp.where(row == column, 1.0, 0.0)
    x = upper_half(error)
    for _ in range(2):
        x = upper_half(error - product(x, x, ((0,), (0,))))
    both = jnp.concatenate([lower, image], axis=1)
    x2 = product(x, x, ((1,), (0,)))
    both = both - product(x, both, ((0,), (0,)))
    both = both + product(x2, both, ((0,), (0,)))
    lower = both[:, :width] * across
    factor[...] = jnp.where(row <= column, both[:, width:] * (1.0 / across), 0.0)
    one, two, three = split(lower.T)
    both = jnp.concatenate([one, two], axis=1)
    both = jnp.concatenate([both, both], axis=0)
    ends = jnp.concatenate([three, one], axis=0)
    load.wait()

    def apply(x, carry):
        rows = block[x]
        q = exact_dot(rows[:, : 2 * width], both)
        small = exact_dot(jnp.concatenate([rows[:, :width], rows[:, 2 * width :]], axis=1), ends)
        q = q[:, :width] + (q[:, width:] + small)
        result[x] = q.reshape(result.shape[1:])
        pltpu.make_async_copy(result.at[x], q_out.at[x], store_sem.at[x]).start()
        return carry

    lax.fori_loop(0, block.shape[0], apply, 0, unroll=True)

    def drain(x, carry):
        pltpu.make_async_copy(result.at[x], q_out.at[x], store_sem.at[x]).wait()
        return carry

    lax.fori_loop(0, block.shape[0], drain, 0)


def local(sizes, orbitals_in, potential):
    bx, by, bz, width = orbitals_in.shape
    points = bx * by * bz * sizes[0] * sizes[1] * sizes[2]
    nx = sizes[0]
    rows = width // 2 // nx
    longest = max(sizes)
    vmem = pl.BlockSpec(memory_space=pltpu.VMEM)
    anywhere = pl.BlockSpec(memory_space=pl.ANY)
    chunk = (2 * rows + 2, width)
    chunks = jax.ShapeDtypeStruct((nx, *chunk), F32)
    slices_shape = jax.ShapeDtypeStruct((bx, by * bz, 3 * width), jnp.bfloat16)
    tiles = (width // 8, 8, width)
    square = jax.ShapeDtypeStruct((width, width), F32)
    pieces, gram = pl.pallas_call(
        functools.partial(filter_kernel, sizes),
        out_shape=(slices_shape, chunks),
        in_specs=[anywhere, anywhere],
        out_specs=(anywhere, vmem),
        scratch_shapes=[
            pltpu.VMEM((bx + 2, by + 2, bz, width), F32),
            pltpu.VMEM((bx + 2, by + 2, bz, width), F32),
            pltpu.VMEM((2, bx, by, width), F32),
            pltpu.VMEM((2, bx, by, width), F32),
            pltpu.VMEM((2, 2, bx, by, width), F32),
            pltpu.VMEM(slices_shape.shape, jnp.bfloat16),
            pltpu.VMEM((bx, by, bz), F32),
            pltpu.VMEM((bx, bz, by), F32),
            pltpu.VMEM((3, width, width), F32),
            pltpu.VMEM(chunks.shape, F32),
            pltpu.VMEM((3, *chunk), F32),
            pltpu.VMEM((3, longest, *chunk), F32),
            pltpu.SemaphoreType.DMA((2,)),
            pltpu.SemaphoreType.DMA(()),
            pltpu.SemaphoreType.DMA((2, 6)),
            pltpu.SemaphoreType.DMA((2, 6)),
            pltpu.SemaphoreType.DMA((4, longest)),
            pltpu.SemaphoreType.DMA((4, longest)),
        ],
        compiler_params=pltpu.CompilerParams(collective_id=0, has_side_effects=True),
        name="filter_gram",
    )(orbitals_in, potential)
    return pl.pallas_call(
        functools.partial(final_kernel, points),
        out_shape=(jax.ShapeDtypeStruct(orbitals_in.shape, F32), square),
        in_specs=[anywhere, vmem],
        out_specs=(anywhere, vmem),
        scratch_shapes=[
            pltpu.VMEM(slices_shape.shape, jnp.bfloat16),
            pltpu.VMEM(tiles, F32),
            pltpu.VMEM(tiles, F32),
            pltpu.VMEM(orbitals_in.shape, F32),
            pltpu.SemaphoreType.DMA(()),
            pltpu.SemaphoreType.DMA((bx,)),
        ],
        name="factor_apply",
    )(pieces, gram)


def solution(mesh):
    sizes = tuple(mesh.shape[a] for a in AXES)
    spec = P("gx", "gy", "gz", None)
    return jax.shard_map(
        functools.partial(local, sizes),
        mesh=mesh,
        in_specs=(spec, P("gx", "gy", "gz")),
        out_specs=(spec, P()),
        check_vma=False,
    )
```
